512 devices in a mesh: blk: 128 (over y, z, core), rep: 4 (over x).
Axes of the slice: x: 4, y: 8, z: 8, core: 2. Of those that a mesh axis runs over, the one named last changes fastest.
Arguments:
- features: bfloat16 [65536, 256], P('blk'), may hold values from -6 to 6
- targets: bfloat16 [65536, 128], P('blk', 'rep'), may hold values from -6 to 6
- conditioning: int32 [512, 2], replicated, may hold values from 0 to 511, as said below
- block_slot: int32 [512], replicated, may hold values from 0 to 511, as said below
Outputs:
- whitened: float32 [65536, 128], P('blk', 'rep')
- grad_features: float32 [65536, 256], P('blk', 'rep')
- grad_targets: float32 [65536, 128], P('blk', 'rep')
The draws below stay inside these ranges and needn't reach their ends.
Inputs may be any that keep to these rules, and one draw needn't show every extreme that they name: `conditioning`: row b lists 2 different blocks among b - 1, b - 2, ..., b - 3, taken modulo 512. `block_slot`: A permutation that keeps each aligned pair of slots 2i, 2i + 1 holding blocks 2i and 2i + 1, in either order; it is its own inverse.
All inputs are finite; a program needn't handle non-finite values.
Results may differ from the reference program's by a relative error of at most 0.0003.
Values may be sent and summed in bfloat16 or wider, within the bound.
No kernel may reach another device: no remote copies, remote signals or barrier semaphores. Data moves between devices by JAX's collectives and lax.ppermute only.
A program may use at most 64 MiB of HBM per device.

```python
import jax
import jax.numpy as jnp
from jax import lax

F = 256
T_SIZE = 128
PTS = 128
NCOND = 2
REACH = 3
NB = 512
ORDER = 384


def draw_conditioning(key, part):
    row_keys = jax.random.split(jax.random.fold_in(key, 11), NB)
    orders = jax.vmap(lambda single: jax.random.permutation(single, REACH))(row_keys)
    steps_back = orders[:, :NCOND].astype(jnp.int32) + 1
    return ((jnp.arange(NB, dtype=jnp.int32)[:, None] - steps_back) % NB).astype(jnp.int32)


def draw_block_slot(key, part):
    swap_bits = jax.random.randint(jax.random.fold_in(key, 23), (NB // 2,), 0, 2, dtype=jnp.int32)
    swap_flags = jnp.repeat(swap_bits, 2)
    base_ids = jnp.arange(NB, dtype=jnp.int32)
    partner = base_ids + 1 - 2 * (base_ids % 2)
    return jnp.where(swap_flags == 1, partner, base_ids).astype(jnp.int32)


def level_of(key, extent, cuts, low, top_value):
    gain, own = 1.0, jax.random.fold_in(key, 6)
    for position, blocks in cuts:
        steps = jnp.exp(jax.random.uniform(jax.random.fold_in(own, position), (blocks,), jnp.float32, low / len(cuts), top_value / len(cuts)))
        gain = gain * jnp.repeat(steps, extent[position] // blocks).reshape([-1 if axis == position else 1 for axis in range(len(extent))])
    return gain


def centred(rng, dims, scale, most, cuts=(), held_as=jnp.bfloat16):
    drawn = jax.random.normal(rng, dims, jnp.float32) * scale
    if len(cuts) > 0:
        drawn = level_of(rng, dims, cuts, -0.22, 0.18) * drawn
    return jnp.clip(drawn, min=-most, max=most).astype(held_as)


def setup_inputs(seed: int = 0) -> dict:
    splits = jax.random.split(jax.random.key(seed), 5)
    return {
        "features": centred(splits[0], (NB * PTS, F), 1.0, 6.0, ((0, 128),)),
        "targets": centred(splits[1], (NB * PTS, T_SIZE), 1.0, 6.0, ((0, 128), (1, 4))),
        "conditioning": draw_conditioning(jax.random.fold_in(splits[4], 71), 0),
        "block_slot": draw_block_slot(jax.random.fold_in(splits[4], 71), 0),
    }


linear_scale = 1.0
gauss_scale = 1.5
nugget = 0.1

def block_loss(gram_matrix, values):
    points = gram_matrix.shape[0]
    squares = jnp.diagonal(gram_matrix)
    distance = squares[:, None] + squares[None, :] - 2.0 * gram_matrix
    kernel = linear_scale * gram_matrix / F + gauss_scale * jnp.exp(-distance / (2.0 * F)) + nugget * jnp.eye(points, dtype=gram_matrix.dtype)
    factor = jnp.linalg.cholesky(kernel)
    solved = jax.scipy.linalg.solve_triangular(factor, values, lower=True)
    whitened = solved[points - PTS:]
    tail_diag = jnp.diagonal(factor)[points - PTS:]
    total_loss = 0.5 * jnp.sum(whitened * whitened) + values.shape[1] * jnp.sum(jnp.log(tail_diag))
    return (total_loss, whitened)

def block_grads(points, values):
    gram_matrix = jnp.dot(points.astype(jnp.float32), points.T.astype(jnp.float32), preferred_element_type=jnp.float32)
    total_loss, pullback, whitened = jax.vjp(block_loss, gram_matrix, values, has_aux=True)
    grad_gram, grad_values = pullback(jnp.ones_like(total_loss))
    grad_points = jnp.dot(grad_gram + grad_gram.T, points.astype(jnp.float32), precision=lax.Precision.HIGHEST)
    return (whitened, grad_points, grad_values)

def reference(features, targets, conditioning, block_slot):
    total_blocks = block_slot.shape[0]
    offsets_in = jnp.arange(PTS, dtype=jnp.int32)

    def per_block(block_id):
        members = jnp.concatenate([conditioning[block_id], block_id[None]]).astype(jnp.int32)
        slot_ids = block_slot[members].astype(jnp.int32)
        rows_index = (slot_ids[:, None] * PTS + offsets_in[None, :]).reshape(-1).astype(jnp.int32)
        points = features[rows_index]
        values = targets[rows_index].astype(jnp.float32)
        whitened, grad_points, grad_values = block_grads(points, values)
        return (whitened, grad_points, grad_values, rows_index)
    whitened, grad_points, grad_values, rows_index = lax.map(per_block, jnp.arange(total_blocks, dtype=jnp.int32))
    own_rows = rows_index[:, ORDER - PTS:]
    whitened_all = jnp.zeros((total_blocks * PTS, targets.shape[1]), jnp.float32).at[own_rows].set(whitened)
    grad_features = jnp.zeros((total_blocks * PTS, features.shape[1]), jnp.float32).at[rows_index].add(grad_points)
    grad_targets = jnp.zeros((total_blocks * PTS, targets.shape[1]), jnp.float32).at[rows_index].add(grad_values)
    return (whitened_all, grad_features, grad_targets)
```

```python
import functools

import jax
import jax.numpy as jnp
from jax import lax
from jax.experimental import pallas as pl
from jax.experimental.pallas import tpu as pltpu
from jax.sharding import PartitionSpec as P

F = 256
PTS = 128
NCOND = 2
T_SIZE = 128
ORDER = PTS * (NCOND + 1)
PANEL = 8
HIGHEST = lax.Precision.HIGHEST

linear_scale = 1.0
gauss_scale = 1.5
nugget = 0.1


def mm(a, b, ca, cb, precision=HIGHEST):
    return lax.dot_general(
        a, b, (((ca,), (cb,)), ((), ())), precision=precision, preferred_element_type=jnp.float32
    )


def splat(value):
    return jnp.broadcast_to(value, (PANEL, PTS))


def inverse_factor(matrix, store):
    count = PTS // PANEL
    lane = lax.broadcasted_iota(jnp.int32, (PANEL, PTS), 1)
    sub = lax.broadcasted_iota(jnp.int32, (PANEL, PTS), 0)
    tiles = [matrix[PANEL * t : PANEL * (t + 1), :] for t in range(count)]
    for j in range(count):
        first = PANEL * j
        tile = tiles[j]
        inside = (lane >= first) & (lane < first + PANEL)
        elem = [
            [splat(tile[i : i + 1, first + k : first + k + 1]) for k in range(i + 1)]
            for i in range(PANEL)
        ]
        held = jnp.where(inside, jnp.where(lane == first + sub, 1.0, 0.0), tile)
        rows = [splat(held[i : i + 1, :]) for i in range(PANEL)]
        recip = []
        for k in range(PANEL):
            recip.append(1.0 / elem[k][k])
            pivots = [elem[m][k] for m in range(k, PANEL)]
            for i in range(k + 1, PANEL):
                scaled = elem[i][k] * recip[k]
                for m in range(k + 1, i + 1):
                    elem[i][m] = elem[i][m] - scaled * pivots[m - k]
                elem[i][k] = scaled
                rows[i] = rows[i] - scaled * rows[k]
        solved = [rows[i] * recip[i] for i in range(PANEL)]
        for k in range(PANEL - 1, 0, -1):
            for i in range(k):
                solved[i] = solved[i] - elem[k][i] * solved[k]
        whole = rows[0] * lax.rsqrt(elem[0][0])
        for i in range(1, PANEL):
            whole = jnp.where(sub == i, rows[i] * lax.rsqrt(elem[i][i]), whole)
        store(first, jnp.where(lane < first + PANEL, whole, 0.0))
        for t in range(j + 1, count):
            left = tiles[t]
            total = jnp.where(inside, 0.0, left)
            for k in range(PANEL):
                total = total - splat(left[:, first + k : first + k + 1]) * solved[k]
            tiles[t] = total


def into(ref, row, col):
    def store(first, value):
        ref[row + first : row + first + PANEL, col : col + PTS] = value

    return store


def member_places(block, cond_ref, slot_ref, blocks, total):
    listed = [cond_ref[m, block] for m in range(NCOND)] + [block]
    places = []
    for other in listed:
        slot = slot_ref[other]
        places.append((slot // blocks != block // blocks, slot % blocks))
    return places


def factor_kernel(blocks, block_ref, cond_ref, slot_ref, prev_ref, own_ref, z_ref, e_ref, la_ref, p_ref):
    block = block_ref[0]
    places = member_places(block, cond_ref, slot_ref, blocks, None)
    for m, (before, place) in enumerate(places):
        rows = pl.ds(pl.multiple_of(place * PTS, PTS), PTS)

        @pl.when(before)
        def _():
            z_ref[m * PTS : (m + 1) * PTS, :] = prev_ref[rows, :]

        @pl.when(jnp.logical_not(before))
        def _():
            z_ref[m * PTS : (m + 1) * PTS, :] = own_ref[rows, :]

    z = z_ref[...]
    gram = mm(z, z, 1, 1, None)
    eye = lax.broadcasted_iota(jnp.int32, (ORDER, ORDER), 0) == lax.broadcasted_iota(
        jnp.int32, (ORDER, ORDER), 1
    )
    diag = jnp.where(eye, gram, 0.0)
    s_row = jnp.sum(diag, axis=0, keepdims=True)
    s_col = jnp.sum(diag, axis=1, keepdims=True)
    gauss = gauss_scale * jnp.exp((s_col + s_row - 2.0 * gram) * (-1.0 / (2.0 * F)))
    e_ref[...] = gauss
    kern = gram * (linear_scale / F) + gauss + jnp.where(eye, nugget, 0.0)

    inverse_factor(kern[:PTS, :PTS], into(la_ref, 0, 0))
    x1 = la_ref[:PTS, :PTS]
    la_ref[:PTS, PTS:] = jnp.zeros((PTS, PTS), jnp.float32)
    t1 = mm(x1, kern[:PTS, PTS:], 1, 0)
    s2 = kern[PTS:, PTS:] - mm(t1, t1, 0, 0)
    inverse_factor(s2[:PTS, :PTS], into(la_ref, PTS, PTS))
    x2 = la_ref[PTS:, PTS:]
    t2 = mm(x2, s2[:PTS, PTS:], 1, 0)
    s3 = s2[PTS:, PTS:] - mm(t2, t2, 0, 0)
    r2 = -mm(x2, mm(t1[:, :PTS], x1, 0, 0), 1, 0)
    la_ref[PTS:, :PTS] = r2
    q1 = mm(t1[:, PTS:], x1, 0, 0) + mm(t2, r2, 0, 0)
    q2 = mm(t2, x2, 0, 0)
    inverse_factor(s3, into(p_ref, 0, 2 * PTS))
    x3 = p_ref[:, 2 * PTS :]
    p_ref[:, :PTS] = -mm(x3, q1, 1, 0)
    p_ref[:, PTS : 2 * PTS] = -mm(x3, q2, 1, 0)


def gradient_kernel(
    blocks, block_ref, cond_ref, slot_ref, prev_ref, own_ref, z_ref, e_ref, la_ref, p_ref, out_ref, y_ref
):
    block = block_ref[0]
    places = member_places(block, cond_ref, slot_ref, blocks, None)
    for m, (before, place) in enumerate(places):
        cols = pl.ds(pl.multiple_of(place * PTS, PTS), PTS)

        @pl.when(before)
        def _():
            y_ref[:, m * PTS : (m + 1) * PTS] = prev_ref[:, cols].astype(jnp.float32)

        @pl.when(jnp.logical_not(before))
        def _():
            y_ref[:, m * PTS : (m + 1) * PTS] = own_ref[:, cols].astype(jnp.float32)

    y = y_ref[...]
    proj = p_ref[...]
    la = la_ref[...]
    white = mm(y, proj, 1, 1)
    delta = mm(white, proj, 1, 0)
    alpha = mm(mm(y[:, : 2 * PTS], la, 1, 1), la, 1, 0)
    half = 0.5 * delta
    beta = jnp.concatenate([half[:, : 2 * PTS] + alpha, half[:, 2 * PTS :]], axis=1)
    left = jnp.concatenate([proj, delta, beta], axis=0)
    right = jnp.concatenate([(0.5 * T_SIZE) * proj, -0.5 * beta, -half], axis=0)
    grad_kern = mm(left, right, 0, 0)
    through = grad_kern * e_ref[...]
    eye = lax.broadcasted_iota(jnp.int32, (ORDER, ORDER), 0) == lax.broadcasted_iota(
        jnp.int32, (ORDER, ORDER), 1
    )
    summed = jnp.sum(through, axis=1, keepdims=True)
    both = (linear_scale * grad_kern + through - jnp.where(eye, summed, 0.0)) * (2.0 / F)
    high = both.astype(jnp.bfloat16)
    low = (both - high.astype(jnp.float32)).astype(jnp.bfloat16)
    z = z_ref[...]
    grad_z = mm(z, high, 0, 0, None) + mm(z, low, 0, 0, None)
    parts = out_ref.shape[0]
    zw = F // parts
    tw = T_SIZE // parts
    for part in range(parts):
        for place, m in enumerate((NCOND,) + tuple(range(NCOND))):
            cols = slice(m * PTS, (m + 1) * PTS)
            row = 0 if place == 0 else zw + 2 * tw + (place - 1) * (zw + tw)
            out_ref[part, row : row + zw, :] = grad_z[part * zw : (part + 1) * zw, cols]
            out_ref[part, row + zw : row + zw + tw, :] = delta[part * tw : (part + 1) * tw, cols]
        out_ref[part, zw + tw : zw + 2 * tw, :] = white[part * tw : (part + 1) * tw, :]


def combine_kernel(blocks, zw, tw, block_ref, cond_ref, slot_ref, got_ref, white_ref, own_ref, prev_ref):
    parts = got_ref.shape[0]
    height = zw + tw
    base = block_ref[0] // blocks * blocks
    own_ref[...] = jnp.zeros_like(own_ref)
    prev_ref[...] = jnp.zeros_like(prev_ref)
    for source in range(parts):
        places = member_places(base + source, cond_ref, slot_ref, blocks, None)
        for m, (before, place) in enumerate(places):
            cols = pl.ds(pl.multiple_of(place * PTS, PTS), PTS)
            row = 0 if m == NCOND else height + tw + m * height
            value = got_ref[source, row : row + height, :]
            if m == NCOND:
                own_ref[:, cols] += value
                white_ref[:, cols] = got_ref[source, height : height + tw, :]
            else:

                @pl.when(before)
                def _():
                    prev_ref[:, cols] += value

                @pl.when(jnp.logical_not(before))
                def _():
                    own_ref[:, cols] += value


def passed_along(value, axis, steps):
    count = lax.axis_size(axis)
    pairs = [(source, (source + steps) % count) for source in range(count)]
    return lax.ppermute(value, axis, pairs)


VMEM = pl.BlockSpec(memory_space=pltpu.VMEM)
SMEM = pl.BlockSpec(memory_space=pltpu.SMEM)


def shape(*dims, dtype=jnp.float32):
    return jax.ShapeDtypeStruct(dims, dtype)


def factor_call(blocks, block, cond, slots, prev, own):
    return pl.pallas_call(
        functools.partial(factor_kernel, blocks),
        out_shape=(
            shape(ORDER, F, dtype=jnp.bfloat16),
            shape(ORDER, ORDER),
            shape(2 * PTS, 2 * PTS),
            shape(PTS, ORDER),
        ),
        in_specs=[SMEM] * 3 + [VMEM] * 2,
        out_specs=(VMEM,) * 4,
        name="factor",
    )(block, cond, slots, prev, own)


def gradient_call(blocks, parts, block, cond, slots, prev, own, z, e, la, p):
    height = 3 * (F + T_SIZE) // parts + T_SIZE // parts
    return pl.pallas_call(
        functools.partial(gradient_kernel, blocks),
        out_shape=shape(parts, height, PTS),
        in_specs=[SMEM] * 3 + [VMEM] * 6,
        out_specs=VMEM,
        scratch_shapes=[pltpu.VMEM((T_SIZE, ORDER), jnp.float32)],
        name="gradient",
    )(block, cond, slots, prev, own, z, e, la, p)


def combine_call(blocks, parts, block, cond, slots, got):
    zw, tw = F // parts, T_SIZE // parts
    rows = blocks * PTS
    return pl.pallas_call(
        functools.partial(combine_kernel, blocks, zw, tw),
        out_shape=(shape(tw, rows), shape(zw + tw, rows), shape(zw + tw, rows)),
        in_specs=[SMEM] * 3 + [VMEM],
        out_specs=(VMEM,) * 3,
        name="combine",
    )(block, cond, slots, got)


def per_device(features, targets, conditioning, block_slot):
    parts = lax.axis_size("rep")
    blocks = features.shape[0] // PTS
    block = (lax.axis_index("blk") * blocks + lax.axis_index("rep")).astype(jnp.int32)[None]
    cond = conditioning.T
    prev_features = passed_along(features, "blk", 1)
    columns = targets.T
    gathered = lax.all_to_all(
        jnp.broadcast_to(columns[None], (parts,) + columns.shape), "rep", 0, 0, tiled=True
    ).reshape(T_SIZE, features.shape[0])
    prev_targets = passed_along(gathered, "blk", 1)
    z, e, la, p = factor_call(blocks, block, cond, block_slot, prev_features, features)
    sent = gradient_call(
        blocks, parts, block, cond, block_slot, prev_targets, gathered, z, e, la, p
    )
    got = lax.all_to_all(sent, "rep", 0, 0, tiled=True)
    white, own, prev = combine_call(blocks, parts, block, cond, block_slot, got)
    own = own + passed_along(prev, "blk", -1)
    zw = F // parts
    return (white.T, own[:zw].T, own[zw:].T)


def solution(mesh):
    in_specs = (P("blk", None), P("blk", "rep"), P(), P())
    out_specs = (P("blk", "rep"), P("blk", "rep"), P("blk", "rep"))
    return jax.shard_map(
        per_device, mesh=mesh, in_specs=in_specs, out_specs=out_specs, check_vma=False
    )
```

```python
import functools

import jax
import jax.numpy as jnp
from jax import lax
from jax.experimental import pallas as pl
from jax.experimental.pallas import tpu as pltpu
from jax.sharding import PartitionSpec as P

F = 256
PTS = 128
NCOND = 2
T_SIZE = 128
ORDER = PTS * (NCOND + 1)
PANEL = 8
HIGHEST = lax.Precision.HIGHEST

linear_scale = 1.0
gauss_scale = 1.5
nugget = 0.1


def mm(a, b, ca, cb, precision=HIGHEST):
    return lax.dot_general(
        a, b, (((ca,), (cb,)), ((), ())), precision=precision, preferred_element_type=jnp.float32
    )


def halves(value):
    high = value.astype(jnp.bfloat16)
    return high, (value - high.astype(jnp.float32)).astype(jnp.bfloat16)


def mm3(a, b, ca, cb):
    (ah, al), (bh, bl) = halves(a), halves(b)
    return mm(ah, bl, ca, cb, None) + mm(al, bh, ca, cb, None) + mm(ah, bh, ca, cb, None)


def splat(value):
    return jnp.broadcast_to(value, (PANEL, PTS))


def across(tile, lane):
    return splat(tile[:, lane : lane + 1])


def down(tile, row):
    return splat(tile[row : row + 1, :])


def inverse_factor(matrix, store):
    count = PTS // PANEL
    lane = lax.broadcasted_iota(jnp.int32, (PANEL, PTS), 1)
    sub = lax.broadcasted_iota(jnp.int32, (PANEL, PTS), 0)
    tiles = [matrix[PANEL * t : PANEL * (t + 1), :] for t in range(count)]
    cols = [across(tiles[0], m) for m in range(PANEL)]
    for j in range(count):
        first = PANEL * j
        more = j + 1 < count
        inside = (lane >= first) & (lane < first + PANEL)
        held = jnp.where(inside, jnp.where(lane == first + sub, 1.0, 0.0), tiles[j])
        if more:
            coef = [across(tiles[j + 1], first + m) for m in range(PANEL)]
            ahead = [across(tiles[j + 1], first + PANEL + m) for m in range(PANEL)]
            after = jnp.where(inside, 0.0, tiles[j + 1])
        recip, lower, rows = [], [], []
        scale = None
        for k in range(PANEL):
            pivot = down(cols[k], k)
            recip.append(1.0 / pivot)
            root = lax.rsqrt(pivot)
            scale = root if scale is None else jnp.where(sub == k, root, scale)
            below = {m: down(cols[k], m) for m in range(k + 1, PANEL)}
            lower.append({m: below[m] * recip[k] for m in below})
            rows.append(down(held, k))
            if below:
                factor = jnp.where(sub > k, cols[k] * recip[k], 0.0)
                for m in below:
                    cols[m] = cols[m] - factor * below[m]
                held = held - factor * rows[k]
            if more:
                factor = coef[k] * recip[k]
                for m in range(PANEL):
                    ahead[m] = ahead[m] - factor * down(coef[k], m)
                for m in below:
                    coef[m] = coef[m] - factor * below[m]
                after = after - factor * rows[k]
        store(first, jnp.where(lane < first + PANEL, held * scale, 0.0))
        if not more:
            break
        if j + 2 < count:
            solved = [rows[i] * recip[i] for i in range(PANEL)]
            for k in range(PANEL - 1, 0, -1):
                for i in range(k):
                    solved[i] = solved[i] - lower[i][k] * solved[k]
        for t in range(j + 2, count):
            total = jnp.where(inside, 0.0, tiles[t])
            for k in range(PANEL):
                total = total - across(tiles[t], first + k) * solved[k]
            tiles[t] = total
        tiles[j + 1] = after
        cols = ahead


def into(ref, row, col):
    def store(first, value):
        ref[row + first : row + first + PANEL, col : col + PTS] = value

    return store


def member_places(block, cond_ref, slot_ref, blocks, total):
    listed = [cond_ref[m, block] for m in range(NCOND)] + [block]
    places = []
    for other in listed:
        slot = slot_ref[other]
        places.append((slot // blocks != block // blocks, slot % blocks))
    return places


def fetch(places, prev_ref, own_ref, into_ref, sems, dim):
    def window(ref, start):
        span = pl.ds(pl.multiple_of(start * PTS, PTS), PTS)
        return ref.at[span, :] if dim == 0 else ref.at[:, span]

    for m, (before, place) in enumerate(places):

        @pl.when(before)
        def _():
            pltpu.make_async_copy(window(prev_ref, place), window(into_ref, m), sems.at[m]).start()

        @pl.when(jnp.logical_not(before))
        def _():
            pltpu.make_async_copy(window(own_ref, place), window(into_ref, m), sems.at[m]).start()

    for m, (before, place) in enumerate(places):
        pltpu.make_async_copy(window(own_ref, place), window(into_ref, m), sems.at[m]).wait()


def factor_kernel(
    blocks, block_ref, cond_ref, slot_ref, prev_ref, own_ref, z_ref, e_ref, la_ref, p_ref, sems
):
    block = block_ref[0]
    places = member_places(block, cond_ref, slot_ref, blocks, None)
    fetch(places, prev_ref, own_ref, z_ref, sems, 0)
    z = z_ref[...]
    gram = mm(z, z, 1, 1, None)
    eye = lax.broadcasted_iota(jnp.int32, (ORDER, ORDER), 0) == lax.broadcasted_iota(
        jnp.int32, (ORDER, ORDER), 1
    )
    diag = jnp.where(eye, gram, 0.0)
    s_row = jnp.sum(diag, axis=0, keepdims=True)
    s_col = jnp.sum(diag, axis=1, keepdims=True)
    gauss = gauss_scale * jnp.exp((s_col + s_row - 2.0 * gram) * (-1.0 / (2.0 * F)))
    e_ref[...] = gauss
    kern = gram * (linear_scale / F) + gauss + jnp.where(eye, nugget, 0.0)

    inverse_factor(kern[:PTS, :PTS], into(la_ref, 0, 0))
    x1 = la_ref[:PTS, :PTS]
    la_ref[:PTS, PTS:] = jnp.zeros((PTS, PTS), jnp.float32)
    k12, k13 = kern[:PTS, PTS : 2 * PTS], kern[:PTS, 2 * PTS :]
    t12 = mm(x1, k12, 1, 0)
    s22 = kern[PTS : 2 * PTS, PTS : 2 * PTS] - mm(t12, t12, 0, 0)
    inverse_factor(s22, into(la_ref, PTS, PTS))
    x2 = la_ref[PTS:, PTS:]
    t13 = mm(x1, k13, 1, 0)
    s23 = kern[PTS : 2 * PTS, 2 * PTS :] - mm(t12, t13, 0, 0)
    s33 = kern[2 * PTS :, 2 * PTS :] - mm(t13, t13, 0, 0)
    u12 = mm(t12, x1, 0, 0)
    u13 = mm(t13, x1, 0, 0)
    t2 = mm(x2, s23, 1, 0)
    s3 = s33 - mm(t2, t2, 0, 0)
    r2 = -mm(x2, u12, 1, 0)
    la_ref[PTS:, :PTS] = r2
    q1 = u13 + mm(t2, r2, 0, 0)
    q2 = mm(t2, x2, 0, 0)
    inverse_factor(s3, into(p_ref, 0, 2 * PTS))
    x3 = p_ref[:, 2 * PTS :]
    p_ref[:, :PTS] = -mm(x3, q1, 1, 0)
    p_ref[:, PTS : 2 * PTS] = -mm(x3, q2, 1, 0)


def gradient_kernel(
    blocks, block_ref, cond_ref, slot_ref, prev_ref, own_ref, z_ref, e_ref, la_ref, p_ref, out_ref, y_ref, sems
):
    block = block_ref[0]
    places = member_places(block, cond_ref, slot_ref, blocks, None)
    fetch(places, prev_ref, own_ref, y_ref, sems, 1)
    y = y_ref[...].astype(jnp.float32)
    proj = p_ref[...]
    la = la_ref[...]
    white = mm3(y, proj, 1, 1)
    delta = mm3(white, proj, 1, 0)
    alpha = mm3(mm3(y[:, : 2 * PTS], la, 1, 1), la, 1, 0)
    half = 0.5 * delta
    beta = jnp.concatenate([half[:, : 2 * PTS] + alpha, half[:, 2 * PTS :]], axis=1)
    left = jnp.concatenate([proj, delta, beta], axis=0)
    right = jnp.concatenate([(0.5 * T_SIZE) * proj, -0.5 * beta, -half], axis=0)
    grad_kern = mm3(left, right, 0, 0)
    through = grad_kern * e_ref[...]
    eye = lax.broadcasted_iota(jnp.int32, (ORDER, ORDER), 0) == lax.broadcasted_iota(
        jnp.int32, (ORDER, ORDER), 1
    )
    summed = jnp.sum(through, axis=1, keepdims=True)
    both = (linear_scale * grad_kern + through - jnp.where(eye, summed, 0.0)) * (2.0 / F)
    high, low = halves(both)
    z = z_ref[...]
    grad_z = mm(z, high, 0, 0, None) + mm(z, low, 0, 0, None)
    parts = out_ref.shape[0]
    zw = F // parts
    tw = T_SIZE // parts
    for part in range(parts):
        for place, m in enumerate((NCOND,) + tuple(range(NCOND))):
            cols = slice(m * PTS, (m + 1) * PTS)
            row = 0 if place == 0 else zw + 2 * tw + (place - 1) * (zw + tw)
            out_ref[part, row : row + zw, :] = grad_z[part * zw : (part + 1) * zw, cols]
            out_ref[part, row + zw : row + zw + tw, :] = delta[part * tw : (part + 1) * tw, cols]
        out_ref[part, zw + tw : zw + 2 * tw, :] = white[part * tw : (part + 1) * tw, :]


def combine_kernel(blocks, zw, tw, block_ref, cond_ref, slot_ref, got_ref, white_ref, own_ref, prev_ref):
    parts = got_ref.shape[0]
    height = zw + tw
    base = block_ref[0] // blocks * blocks
    own_ref[...] = jnp.zeros_like(own_ref)
    prev_ref[...] = jnp.zeros_like(prev_ref)
    for source in range(parts):
        places = member_places(base + source, cond_ref, slot_ref, blocks, None)
        for m, (before, place) in enumerate(places):
            cols = pl.ds(pl.multiple_of(place * PTS, PTS), PTS)
            row = 0 if m == NCOND else height + tw + m * height
            value = got_ref[source, row : row + height, :]
            if m == NCOND:
                own_ref[:, cols] += value
                white_ref[:, cols] = got_ref[source, height : height + tw, :]
            else:

                @pl.when(before)
                def _():
                    prev_ref[:, cols] += value

                @pl.when(jnp.logical_not(before))
                def _():
                    own_ref[:, cols] += value


def passed_along(value, axis, steps):
    count = lax.axis_size(axis)
    pairs = [(source, (source + steps) % count) for source in range(count)]
    return lax.ppermute(value, axis, pairs)


VMEM = pl.BlockSpec(memory_space=pltpu.VMEM)
SMEM = pl.BlockSpec(memory_space=pltpu.SMEM)
ANY = pl.BlockSpec(memory_space=pl.ANY)


def shape(*dims, dtype=jnp.float32):
    return jax.ShapeDtypeStruct(dims, dtype)


def factor_call(blocks, block, cond, slots, prev, own):
    return pl.pallas_call(
        functools.partial(factor_kernel, blocks),
        out_shape=(
            shape(ORDER, F, dtype=jnp.bfloat16),
            shape(ORDER, ORDER),
            shape(2 * PTS, 2 * PTS),
            shape(PTS, ORDER),
        ),
        in_specs=[SMEM] * 3 + [ANY] * 2,
        out_specs=(VMEM,) * 4,
        scratch_shapes=[pltpu.SemaphoreType.DMA((NCOND + 1,))],
        name="factor",
    )(block, cond, slots, prev, own)


def gradient_call(blocks, parts, block, cond, slots, prev, own, z, e, la, p):
    height = 3 * (F + T_SIZE) // parts + T_SIZE // parts
    return pl.pallas_call(
        functools.partial(gradient_kernel, blocks),
        out_shape=shape(parts, height, PTS),
        in_specs=[SMEM] * 3 + [ANY] * 2 + [VMEM] * 4,
        out_specs=VMEM,
        scratch_shapes=[
            pltpu.VMEM((T_SIZE, ORDER), jnp.bfloat16),
            pltpu.SemaphoreType.DMA((NCOND + 1,)),
        ],
        name="gradient",
    )(block, cond, slots, prev, own, z, e, la, p)


def combine_call(blocks, parts, block, cond, slots, got):
    zw, tw = F // parts, T_SIZE // parts
    rows = blocks * PTS
    return pl.pallas_call(
        functools.partial(combine_kernel, blocks, zw, tw),
        out_shape=(shape(tw, rows), shape(zw + tw, rows), shape(zw + tw, rows)),
        in_specs=[SMEM] * 3 + [VMEM],
        out_specs=(VMEM,) * 3,
        name="combine",
    )(block, cond, slots, got)


def sum_kernel(own_ref, more_ref, z_ref, y_ref):
    zw = z_ref.shape[0]
    z_ref[...] = own_ref[:zw, :] + more_ref[:zw, :]
    y_ref[...] = own_ref[zw:, :] + more_ref[zw:, :]


def sum_call(parts, own, more):
    rows = own.shape[1]
    return pl.pallas_call(
        sum_kernel,
        out_shape=(shape(F // parts, rows), shape(T_SIZE // parts, rows)),
        in_specs=[VMEM] * 2,
        out_specs=(VMEM,) * 2,
        name="total",
    )(own, more)


def per_device(features, targets, conditioning, block_slot):
    parts = lax.axis_size("rep")
    blocks = features.shape[0] // PTS
    block = (lax.axis_index("blk") * blocks + lax.axis_index("rep")).astype(jnp.int32)[None]
    cond = conditioning.T
    prev_features = passed_along(features, "blk", 1)
    columns = targets.T
    gathered = lax.all_to_all(
        jnp.broadcast_to(columns[None], (parts,) + columns.shape), "rep", 0, 0, tiled=True
    ).reshape(T_SIZE, features.shape[0])
    prev_targets = passed_along(gathered, "blk", 1)
    z, e, la, p = factor_call(blocks, block, cond, block_slot, prev_features, features)
    sent = gradient_call(
        blocks, parts, block, cond, block_slot, prev_targets, gathered, z, e, la, p
    )
    got = lax.all_to_all(sent, "rep", 0, 0, tiled=True)
    white, own, prev = combine_call(blocks, parts, block, cond, block_slot, got)
    grad_z, grad_y = sum_call(parts, own, passed_along(prev, "blk", -1))
    return (white.T, grad_z.T, grad_y.T)


def solution(mesh):
    in_specs = (P("blk", None), P("blk", "rep"), P(), P())
    out_specs = (P("blk", "rep"), P("blk", "rep"), P("blk", "rep"))
    return jax.shard_map(
        per_device, mesh=mesh, in_specs=in_specs, out_specs=out_specs, check_vma=False
    )
```

```python
import functools

import jax
import jax.numpy as jnp
from jax import lax
from jax.experimental import pallas as pl
from jax.experimental.pallas import tpu as pltpu
from jax.sharding import PartitionSpec as P

F = 256
PTS = 128
NCOND = 2
T_SIZE = 128
ORDER = PTS * (NCOND + 1)
PANEL = 8
HIGHEST = lax.Precision.HIGHEST

linear_scale = 1.0
gauss_scale = 1.5
nugget = 0.1


def mm(a, b, ca, cb, precision=HIGHEST):
    return lax.dot_general(
        a, b, (((ca,), (cb,)), ((), ())), precision=precision, preferred_element_type=jnp.float32
    )


def halves(value):
    high = value.astype(jnp.bfloat16)
    return high, (value - high.astype(jnp.float32)).astype(jnp.bfloat16)


def mm3(a, b, ca, cb):
    (ah, al), (bh, bl) = halves(a), halves(b)
    return mm(ah, bl, ca, cb, None) + mm(al, bh, ca, cb, None) + mm(ah, bh, ca, cb, None)


def splat(value):
    return jnp.broadcast_to(value, (PANEL, PTS))


def across(tile, lane):
    return splat(tile[:, lane : lane + 1])


def down(tile, row):
    return splat(tile[row : row + 1, :])


def inverse_factor(matrix, store):
    count = PTS // PANEL
    lane = lax.broadcasted_iota(jnp.int32, (PANEL, PTS), 1)
    sub = lax.broadcasted_iota(jnp.int32, (PANEL, PTS), 0)
    tiles = [matrix[PANEL * t : PANEL * (t + 1), :] for t in range(count)]
    cols = [across(tiles[0], m) for m in range(PANEL)]
    for j in range(count):
        first = PANEL * j
        more = j + 1 < count
        inside = (lane >= first) & (lane < first + PANEL)
        held = jnp.where(inside, jnp.where(lane == first + sub, 1.0, 0.0), tiles[j])
        if more:
            coef = [across(tiles[j + 1], first + m) for m in range(PANEL)]
            ahead = [across(tiles[j + 1], first + PANEL + m) for m in range(PANEL)]
            after = jnp.where(inside, 0.0, tiles[j + 1])
        recip, lower, rows = [], [], []
        scale = None
        for k in range(PANEL):
            pivot = down(cols[k], k)
            recip.append(1.0 / pivot)
            root = lax.rsqrt(pivot)
            scale = root if scale is None else jnp.where(sub == k, root, scale)
            below = {m: down(cols[k], m) for m in range(k + 1, PANEL)}
            lower.append({m: below[m] * recip[k] for m in below})
            rows.append(down(held, k))
            if below:
                factor = jnp.where(sub > k, cols[k] * recip[k], 0.0)
                for m in below:
                    cols[m] = cols[m] - factor * below[m]
                held = held - factor * rows[k]
            if more:
                factor = coef[k] * recip[k]
                for m in range(PANEL):
                    ahead[m] = ahead[m] - factor * down(coef[k], m)
                for m in below:
                    coef[m] = coef[m] - factor * below[m]
                after = after - factor * rows[k]
        store(first, jnp.where(lane < first + PANEL, held * scale, 0.0))
        if not more:
            break
        if j + 2 < count:
            solved = [rows[i] * recip[i] for i in range(PANEL)]
            for k in range(PANEL - 1, 0, -1):
                for i in range(k):
                    solved[i] = solved[i] - lower[i][k] * solved[k]
        for t in range(j + 2, count):
            total = jnp.where(inside, 0.0, tiles[t])
            for k in range(PANEL):
                total = total - across(tiles[t], first + k) * solved[k]
            tiles[t] = total
        tiles[j + 1] = after
        cols = ahead


def into(ref, row, col):
    def store(first, value):
        ref[row + first : row + first + PANEL, col : col + PTS] = value

    return store


def member_places(block, cond_ref, slot_ref, blocks, total):
    listed = [cond_ref[m, block] for m in range(NCOND)] + [block]
    places = []
    for other in listed:
        slot = slot_ref[other]
        places.append((slot // blocks != block // blocks, slot % blocks))
    return places


def fetch(places, prev_ref, own_ref, into_ref, sems, dim):
    def window(ref, start):
        span = pl.ds(pl.multiple_of(start * PTS, PTS), PTS)
        return ref.at[span, :] if dim == 0 else ref.at[:, span]

    for m, (before, place) in enumerate(places):

        @pl.when(before)
        def _():
            pltpu.make_async_copy(window(prev_ref, place), window(into_ref, m), sems.at[m]).start()

        @pl.when(jnp.logical_not(before))
        def _():
            pltpu.make_async_copy(window(own_ref, place), window(into_ref, m), sems.at[m]).start()

    for m, (before, place) in enumerate(places):
        pltpu.make_async_copy(window(own_ref, place), window(into_ref, m), sems.at[m]).wait()


def factor_kernel(
    blocks, block_ref, cond_ref, slot_ref, prev_ref, own_ref, z_ref, e_ref, la_ref, p_ref, sems
):
    block = block_ref[0]
    places = member_places(block, cond_ref, slot_ref, blocks, None)
    fetch(places, prev_ref, own_ref, z_ref, sems, 0)
    z = z_ref[...]
    gram = mm(z, z, 1, 1, None)
    eye = lax.broadcasted_iota(jnp.int32, (ORDER, ORDER), 0) == lax.broadcasted_iota(
        jnp.int32, (ORDER, ORDER), 1
    )
    diag = jnp.where(eye, gram, 0.0)
    s_row = jnp.sum(diag, axis=0, keepdims=True)
    s_col = jnp.sum(diag, axis=1, keepdims=True)
    gauss = gauss_scale * jnp.exp((s_col + s_row - 2.0 * gram) * (-1.0 / (2.0 * F)))
    e_ref[...] = gauss
    kern = gram * (linear_scale / F) + gauss + jnp.where(eye, nugget, 0.0)

    inverse_factor(kern[:PTS, :PTS], into(la_ref, 0, 0))
    x1 = la_ref[:PTS, :PTS]
    la_ref[:PTS, PTS:] = jnp.zeros((PTS, PTS), jnp.float32)
    k12, k13 = kern[:PTS, PTS : 2 * PTS], kern[:PTS, 2 * PTS :]
    t12 = mm(x1, k12, 1, 0)
    s22 = kern[PTS : 2 * PTS, PTS : 2 * PTS] - mm(t12, t12, 0, 0)
    inverse_factor(s22, into(la_ref, PTS, PTS))
    x2 = la_ref[PTS:, PTS:]
    t13 = mm(x1, k13, 1, 0)
    s23 = kern[PTS : 2 * PTS, 2 * PTS :] - mm(t12, t13, 0, 0)
    s33 = kern[2 * PTS :, 2 * PTS :] - mm(t13, t13, 0, 0)
    u12 = mm(t12, x1, 0, 0)
    u13 = mm(t13, x1, 0, 0)
    t2 = mm(x2, s23, 1, 0)
    s3 = s33 - mm(t2, t2, 0, 0)
    r2 = -mm(x2, u12, 1, 0)
    la_ref[PTS:, :PTS] = r2
    q1 = u13 + mm(t2, r2, 0, 0)
    q2 = mm(t2, x2, 0, 0)
    inverse_factor(s3, into(p_ref, 0, 2 * PTS))
    x3 = p_ref[:, 2 * PTS :]
    p_ref[:, :PTS] = -mm(x3, q1, 1, 0)
    p_ref[:, PTS : 2 * PTS] = -mm(x3, q2, 1, 0)


def gradient_kernel(
    blocks, block_ref, cond_ref, slot_ref, prev_ref, own_ref, z_ref, e_ref, la_ref, p_ref, out_ref, y_ref, sems
):
    block = block_ref[0]
    places = member_places(block, cond_ref, slot_ref, blocks, None)
    fetch(places, prev_ref, own_ref, y_ref, sems, 1)
    y = y_ref[...].astype(jnp.float32)
    proj = p_ref[...]
    la = la_ref[...]
    white = mm3(y, proj, 1, 1)
    delta = mm3(white, proj, 1, 0)
    alpha = mm3(mm3(y[:, : 2 * PTS], la, 1, 1), la, 1, 0)
    half = 0.5 * delta
    beta = jnp.concatenate([half[:, : 2 * PTS] + alpha, half[:, 2 * PTS :]], axis=1)
    left = jnp.concatenate([proj, delta, beta], axis=0)
    right = jnp.concatenate([(0.5 * T_SIZE) * proj, -0.5 * beta, -half], axis=0)
    grad_kern = mm3(left, right, 0, 0)
    through = grad_kern * e_ref[...]
    eye = lax.broadcasted_iota(jnp.int32, (ORDER, ORDER), 0) == lax.broadcasted_iota(
        jnp.int32, (ORDER, ORDER), 1
    )
    summed = jnp.sum(through, axis=1, keepdims=True)
    both = (linear_scale * grad_kern + through - jnp.where(eye, summed, 0.0)) * (2.0 / F)
    high, low = halves(both)
    z = z_ref[...]
    grad_z = mm(z, high, 0, 0, None) + mm(z, low, 0, 0, None)
    parts = out_ref.shape[0]
    zw = F // parts
    tw = T_SIZE // parts
    for part in range(parts):
        for place, m in enumerate((NCOND,) + tuple(range(NCOND))):
            cols = slice(m * PTS, (m + 1) * PTS)
            row = 0 if place == 0 else zw + 2 * tw + (place - 1) * (zw + tw)
            out_ref[part, row : row + zw, :] = grad_z[part * zw : (part + 1) * zw, cols]
            out_ref[part, row + zw : row + zw + tw, :] = delta[part * tw : (part + 1) * tw, cols]
        out_ref[part, zw + tw : zw + 2 * tw, :] = white[part * tw : (part + 1) * tw, :]


def combine_kernel(
    blocks, zw, tw, block_ref, cond_ref, slot_ref, got_ref, white_ref, z_ref, y_ref, prev_ref
):
    parts = got_ref.shape[0]
    height = zw + tw
    base = block_ref[0] // blocks * blocks
    z_ref[...] = jnp.zeros_like(z_ref)
    y_ref[...] = jnp.zeros_like(y_ref)
    prev_ref[...] = jnp.zeros_like(prev_ref)
    for source in range(parts):
        places = member_places(base + source, cond_ref, slot_ref, blocks, None)
        for m, (before, place) in enumerate(places):
            cols = pl.ds(pl.multiple_of(place * PTS, PTS), PTS)
            row = 0 if m == NCOND else height + tw + m * height
            value = got_ref[source, row : row + height, :]
            if m == NCOND:
                z_ref[:, cols] += value[:zw]
                y_ref[:, cols] += value[zw:]
                white_ref[:, cols] = got_ref[source, height : height + tw, :]
            else:

                @pl.when(before)
                def _():
                    prev_ref[:, cols] += value

                @pl.when(jnp.logical_not(before))
                def _():
                    z_ref[:, cols] += value[:zw]
                    y_ref[:, cols] += value[zw:]


def near(*values):
    kept = tuple(pltpu.with_memory_space_constraint(value, pltpu.VMEM) for value in values)
    return kept if len(kept) > 1 else kept[0]


def passed_along(value, axis, steps):
    count = lax.axis_size(axis)
    pairs = [(source, (source + steps) % count) for source in range(count)]
    return lax.ppermute(value, axis, pairs)


VMEM = pl.BlockSpec(memory_space=pltpu.VMEM)
SMEM = pl.BlockSpec(memory_space=pltpu.SMEM)
ANY = pl.BlockSpec(memory_space=pl.ANY)


def shape(*dims, dtype=jnp.float32):
    return jax.ShapeDtypeStruct(dims, dtype)


def factor_call(blocks, block, cond, slots, prev, own):
    return pl.pallas_call(
        functools.partial(factor_kernel, blocks),
        out_shape=(
            shape(ORDER, F, dtype=jnp.bfloat16),
            shape(ORDER, ORDER),
            shape(2 * PTS, 2 * PTS),
            shape(PTS, ORDER),
        ),
        in_specs=[SMEM] * 3 + [ANY] * 2,
        out_specs=(VMEM,) * 4,
        scratch_shapes=[pltpu.SemaphoreType.DMA((NCOND + 1,))],
        name="factor",
    )(block, cond, slots, prev, own)


def gradient_call(blocks, parts, block, cond, slots, prev, own, z, e, la, p):
    height = 3 * (F + T_SIZE) // parts + T_SIZE // parts
    return pl.pallas_call(
        functools.partial(gradient_kernel, blocks),
        out_shape=shape(parts, height, PTS),
        in_specs=[SMEM] * 3 + [ANY] * 2 + [VMEM] * 4,
        out_specs=VMEM,
        scratch_shapes=[
            pltpu.VMEM((T_SIZE, ORDER), jnp.bfloat16),
            pltpu.SemaphoreType.DMA((NCOND + 1,)),
        ],
        name="gradient",
    )(block, cond, slots, prev, own, z, e, la, p)


def combine_call(blocks, parts, block, cond, slots, got):
    zw, tw = F // parts, T_SIZE // parts
    rows = blocks * PTS
    return pl.pallas_call(
        functools.partial(combine_kernel, blocks, zw, tw),
        out_shape=(shape(tw, rows), shape(zw, rows), shape(tw, rows), shape(zw + tw, rows)),
        in_specs=[SMEM] * 3 + [VMEM],
        out_specs=(VMEM,) * 4,
        name="combine",
    )(block, cond, slots, got)


def per_device(features, targets, conditioning, block_slot):
    parts = lax.axis_size("rep")
    blocks = features.shape[0] // PTS
    block = (lax.axis_index("blk") * blocks + lax.axis_index("rep")).astype(jnp.int32)[None]
    cond = conditioning.T
    prev_features = near(passed_along(features, "blk", 1))
    columns = targets.T
    gathered = lax.all_to_all(
        jnp.broadcast_to(columns[None], (parts,) + columns.shape), "rep", 0, 0, tiled=True
    ).reshape(T_SIZE, features.shape[0])
    prev_targets = near(passed_along(gathered, "blk", 1))
    z, e, la, p = factor_call(blocks, block, cond, block_slot, prev_features, features)
    sent = gradient_call(
        blocks, parts, block, cond, block_slot, prev_targets, gathered, z, e, la, p
    )
    got = lax.all_to_all(sent, "rep", 0, 0, tiled=True)
    white, own_z, own_y, prev = combine_call(blocks, parts, block, cond, block_slot, got)
    more = passed_along(prev, "blk", -1)
    zw = F // parts
    return (white.T, (own_z + more[:zw]).T, (own_y + more[zw:]).T)


def solution(mesh):
    in_specs = (P("blk", None), P("blk", "rep"), P(), P())
    out_specs = (P("blk", "rep"), P("blk", "rep"), P("blk", "rep"))
    return jax.shard_map(
        per_device, mesh=mesh, in_specs=in_specs, out_specs=out_specs, check_vma=False
    )
```
